256 devices in a mesh: seg: 32 (over y, x, core), band: 8 (over z).
Axes of the slice: x: 4, y: 4, z: 8, core: 2. Of those that a mesh axis runs over, the one named last changes fastest.
Arguments:
- jac_first: bfloat16 [32, 4, 4096, 384], P('seg', None, 'band'), may hold values from -0.09375 to 0.09375
- jac_second: bfloat16 [32, 4, 4096, 384], P('seg', None, 'band'), may hold values from -0.013671875 to 0.013671875
- residual: bfloat16 [32, 4, 4096], P('seg', None, 'band'), may hold values from -1.25 to 1.25
- damp_inner: float32 [32, 3, 384], P('seg'), may hold values from 0.01 to 0.05
- damp_sep: float32 [32, 384], P('seg'), may hold values from 0.01 to 0.05
Outputs:
- separators: float32 [32, 384], P('seg')
- interior: float32 [32, 3, 384], P('seg')
The draws below stay inside these ranges and needn't reach their ends.
All inputs are finite; a program needn't handle non-finite values.
Results may differ from the reference program's by a relative error of at most 0.0003.
Values may be sent and summed in bfloat16 or wider, within the bound.
No kernel may reach another device: no remote copies, remote signals or barrier semaphores. Data moves between devices by JAX's collectives and lax.ppermute only.
A program may use at most 128 MiB of HBM per device.

```python
import math
import jax
import jax.numpy as jnp
from jax import lax

P_SIZE = 384
KB = 3
ROWS = 4096
LINKS = 4
SEGS = 32


def shard_levels(own_key, extent, shards, smallest, high):
    def one(dim, parts):
        steps = jax.random.uniform(jax.random.fold_in(jax.random.fold_in(own_key, 6), dim), (parts,), jnp.float32, smallest / len(shards), high / len(shards))
        return jnp.repeat(jnp.exp(steps), extent[dim] // parts).reshape((-1,) + (1,) * (len(extent) - dim - 1))

    factor_of = one(*shards[0])
    for cut in shards[1:]:
        factor_of = factor_of * one(*cut)
    return factor_of


def noise(stream_key, dims, scale, bound, shards=(), dtype=jnp.bfloat16):
    gain = shard_levels(stream_key, dims, shards, -0.22, 0.18) if shards else 1.0
    result = jax.random.normal(stream_key, dims, jnp.float32) * scale * gain
    return jnp.minimum(jnp.maximum(result, -bound), bound).astype(dtype)


def setup_inputs(seed: int = 0) -> dict:
    streams_of = jax.random.split(jax.random.key(seed), 6)
    jac_first = noise(streams_of[0], (SEGS, LINKS, ROWS, P_SIZE), ROWS ** -0.5, 0.09375, ((0, 32), (2, 8)))
    jac_second = noise(streams_of[1], (SEGS, LINKS, ROWS, P_SIZE), (0.15 / ROWS ** 0.5), 0.013671875, ((0, 32), (2, 8)))
    residual = noise(streams_of[2], (SEGS, LINKS, ROWS), 0.2, 1.25, ((0, 32), (2, 8)))
    damp_inner = jnp.clip(jnp.exp(math.log(0.05) - 1.609438 * jax.random.uniform(streams_of[3], (SEGS, KB, P_SIZE), jnp.float32) ** shard_levels(streams_of[3], (SEGS, KB, P_SIZE), ((0, 32),), -0.2, 0.2)), 0.01, 0.05)
    damp_sep = jnp.clip(jnp.exp(math.log(0.05) - 1.609438 * jax.random.uniform(streams_of[4], (SEGS, P_SIZE), jnp.float32) ** shard_levels(streams_of[4], (SEGS, P_SIZE), ((0, 32),), -0.2, 0.2)), 0.01, 0.05)
    return dict(jac_first=jac_first, jac_second=jac_second, residual=residual, damp_inner=damp_inner, damp_sep=damp_sep)


HIGH = lax.Precision.HIGHEST

def matmul_high(left, right):
    return jnp.matmul(left, right, precision=HIGH)

def lower_solve(chol, rhs):
    return jax.scipy.linalg.solve_triangular(chol, rhs, lower=True)

def upper_solve(chol, rhs):
    return jax.scipy.linalg.solve_triangular(chol, rhs, lower=True, trans=1)

def link_tiles(first, second, resid):
    first = first.astype(jnp.float32)
    second = second.astype(jnp.float32)
    resid = resid.astype(jnp.float32)
    paa = jnp.einsum('lri,lrj->lij', first, first, precision=HIGH)
    pab = jnp.einsum('lri,lrj->lij', first, second, precision=HIGH)
    pbb = jnp.einsum('lri,lrj->lij', second, second, precision=HIGH)
    grad_a = jnp.einsum('lri,lr->li', first, resid, precision=HIGH)
    grad_b = jnp.einsum('lri,lr->li', second, resid, precision=HIGH)
    size = paa.shape[-1]
    zero_tile = jnp.zeros((1, size, size), jnp.float32)
    zero_row = jnp.zeros((1, size), jnp.float32)
    diag = jnp.concatenate([paa, zero_tile]) + jnp.concatenate([zero_tile, pbb - pab - jnp.swapaxes(pab, 1, 2) + paa])
    off = pab - paa
    grad = jnp.concatenate([grad_a, zero_row]) + jnp.concatenate([zero_row, grad_b - grad_a])
    return (diag, off, grad)

def segment_complement(diag, off, grad, damp_inner, damp_sep):
    size = diag.shape[-1]
    inner = damp_inner.shape[0]
    chols, lows, zlist, wlist = ([], [], [], [])
    zero = jnp.zeros((size, size), jnp.float32)
    for k in range(inner):
        block = diag[k + 1] + jnp.diag(damp_inner[k])
        left = off[0].T if k == 0 else zero
        right = off[inner] if k == inner - 1 else zero
        couple = jnp.concatenate([left, right], axis=1)
        target = -grad[k + 1]
        if k > 0:
            block = block - matmul_high(lows[-1], lows[-1].T)
            couple = couple - matmul_high(lows[-1], zlist[-1])
            target = target - matmul_high(lows[-1], wlist[-1])
        chol = jnp.linalg.cholesky(block)
        zlist.append(lower_solve(chol, couple))
        wlist.append(lower_solve(chol, target))
        chols.append(chol)
        if k < inner - 1:
            lows.append(lower_solve(chol, off[k + 1]).T)
    top = jnp.concatenate([diag[0], zero], axis=1)
    bottom = jnp.concatenate([zero, diag[inner + 1] + jnp.diag(damp_sep)], axis=1)
    schur = jnp.concatenate([top, bottom], axis=0)
    reduced = jnp.concatenate([-grad[0], -grad[inner + 1]])
    for k in range(inner):
        schur = schur - matmul_high(zlist[k].T, zlist[k])
        reduced = reduced - matmul_high(zlist[k].T, wlist[k])
    comp = (schur[:size, :size], schur[:size, size:], schur[size:, size:], reduced[:size], reduced[size:])
    return (comp, (chols, lows, zlist, wlist))

def back_substitute(factors, left, right):
    chols, lows, zlist, wlist = factors
    inner = len(chols)
    ends = jnp.concatenate([left, right])
    values = [wlist[k] - matmul_high(zlist[k], ends) for k in range(inner)]
    steps = [None] * inner
    steps[inner - 1] = upper_solve(chols[inner - 1], values[inner - 1])
    for k in range(inner - 2, -1, -1):
        steps[k] = upper_solve(chols[k], values[k] - matmul_high(lows[k].T, steps[k + 1]))
    return jnp.stack(steps)

def merge(first_arc, second_arc):
    all_a, alr_a, arr_a, al_a, ar_a = first_arc
    bll, blr, brr, bl, br = second_arc
    size = all_a.shape[0]
    chol = jnp.linalg.cholesky(arr_a + bll)
    couple = jnp.concatenate([alr_a.T, blr], axis=1)
    weights = jax.scipy.linalg.cho_solve((chol, True), couple)
    shifted = jax.scipy.linalg.cho_solve((chol, True), ar_a + bl)
    new_ll = all_a - matmul_high(alr_a, weights[:, :size])
    new_lr = -matmul_high(alr_a, weights[:, size:])
    new_rr = brr - matmul_high(blr.T, weights[:, size:])
    new_l = al_a - matmul_high(alr_a, shifted)
    new_r = br - matmul_high(blr.T, shifted)
    return ((new_ll, new_lr, new_rr, new_l, new_r), (weights, shifted))

def closure(arc):
    all_a, alr_a, arr_a, al_a, ar_a = arc
    whole = all_a + alr_a + alr_a.T + arr_a
    chol = jnp.linalg.cholesky(whole)
    return jax.scipy.linalg.cho_solve((chol, True), al_a + ar_a)

def middle_step(saved, left, right):
    weights, shifted = saved
    size = left.shape[0]
    return shifted - matmul_high(weights[:, :size], left) - matmul_high(weights[:, size:], right)

def one_segment(items):
    first, second, resid, inner_damp, sep_damp = items
    diag, off, grad = link_tiles(first, second, resid)
    return segment_complement(diag, off, grad, inner_damp, sep_damp)

def reference(jac_first, jac_second, residual, damp_inner, damp_sep):
    comps, factors = lax.map(one_segment, (jac_first, jac_second, residual, damp_inner, damp_sep))
    count = jac_first.shape[0]
    levels = count.bit_length() - 1
    arcs = comps
    saved_all = []
    for level in range(levels):
        even = jax.tree.map(lambda item: item[0::2], arcs)
        odd = jax.tree.map(lambda item: item[1::2], arcs)
        arcs, saved = jax.vmap(merge)(even, odd)
        saved_all.append(saved)
    top = closure(jax.tree.map(lambda item: item[0], arcs))
    lefts = top[None]
    rights = top[None]
    for level in range(levels - 1, -1, -1):
        middles = jax.vmap(middle_step)(saved_all[level], lefts, rights)
        lefts = jnp.stack([lefts, middles], axis=1).reshape(-1, top.shape[0])
        rights = jnp.stack([middles, rights], axis=1).reshape(-1, top.shape[0])

    def solve_inner(items):
        factor, left, right = items
        return back_substitute(factor, left, right)
    interior = lax.map(solve_inner, (factors, lefts, rights))
    return (rights, interior)
```

```python
import functools
import jax
import jax.numpy as jnp
from jax import lax
from jax.experimental import pallas as pl
from jax.experimental.pallas import tpu as pltpu
from jax.sharding import PartitionSpec as P

HIGH = lax.Precision.HIGHEST
B = 128
f32 = jnp.float32
VMEM = pl.BlockSpec(memory_space=pltpu.VMEM)
PARAMS = pltpu.CompilerParams(vmem_limit_bytes=48 << 20)


def dg(a, b, ca, cb):
    return lax.dot_general(a, b, (((ca,), (cb,)), ((), ())), precision=HIGH, preferred_element_type=f32)


def nn(a, b):
    return dg(a, b, 1, 0)


def nt(a, b):
    return dg(a, b, 1, 1)


def tn(a, b):
    return dg(a, b, 0, 0)


def iota2(shape):
    return lax.broadcasted_iota(jnp.int32, shape, 0), lax.broadcasted_iota(jnp.int32, shape, 1)


def inverse_factors(mats):
    mats = [[m[8 * i : 8 * i + 8, :] for i in range(B // 8)] for m in mats]
    sub, lane = iota2((8, B))
    wide = lambda x: jnp.broadcast_to(x, (8, B))
    for p in range(B // 8):
        k = 8 * p
        panel = (lane >= k) & (lane < k + 8)
        eye = jnp.where(lane == sub + k, 1.0, 0.0)
        state = []
        for m in mats:
            cols = [wide(m[p][:, k + j : k + j + 1]) for j in range(8)]
            g = {(i, j): wide(cols[j][i : i + 1, :]) for j in range(8) for i in range(j, 8)}
            start = jnp.where(panel, eye, m[p])
            r = [wide(start[j : j + 1, :]) for j in range(8)]
            state.append((g, r, [None] * 8, {}))
        for j in range(8):
            for g, r, inv, l in state:
                inv[j] = 1.0 / g[j, j]
            for g, r, inv, l in state:
                for i in range(j + 1, 8):
                    l[i, j] = g[i, j] * inv[j]
                for i in range(j + 1, 8):
                    for h in range(i, 8):
                        g[h, i] = g[h, i] - l[h, j] * g[i, j]
                for i in range(j + 1, 8):
                    r[i] = r[i] - l[i, j] * r[j]
        solved = []
        for g, r, inv, l in state:
            y = [None] * 8
            for j in range(7, -1, -1):
                acc = r[j] * inv[j]
                for i in range(7, j, -1):
                    acc = acc - l[i, j] * y[i]
                y[j] = acc
            solved.append(y)
        for i in range(p + 1, B // 8):
            for m, y in zip(mats, solved):
                c = [wide(m[i][:, k + j : k + j + 1]) for j in range(8)]
                even = c[0] * y[0]
                odd = c[1] * y[1]
                for j in range(2, 8, 2):
                    even = even + c[j] * y[j]
                    odd = odd + c[j + 1] * y[j + 1]
                m[i] = jnp.where(panel, 0.0, m[i]) - (even + odd)
        for m, (g, r, inv, l) in zip(mats, state):
            out = r[0] * lax.rsqrt(g[0, 0])
            for j in range(1, 8):
                out = jnp.where(sub == j, r[j] * lax.rsqrt(g[j, j]), out)
            m[p] = jnp.where(lane < k + 8, out, 0.0)
    return [jnp.concatenate(m, axis=0) for m in mats]


def factor(blocks, stores):
    n = range(len(blocks))
    zero = jnp.zeros((B, B), f32)
    x11 = inverse_factors([blocks[q](0, 0) for q in n])
    w21 = [nt(blocks[q](1, 0), x11[q]) for q in n]
    w31 = [nt(blocks[q](2, 0), x11[q]) for q in n]
    s22 = [blocks[q](1, 1) - nt(w21[q], w21[q]) for q in n]
    s32 = [blocks[q](2, 1) - nt(w31[q], w21[q]) for q in n]
    s33 = [blocks[q](2, 2) - nt(w31[q], w31[q]) for q in n]
    x22 = inverse_factors(s22)
    w32 = [nt(s32[q], x22[q]) for q in n]
    s33 = [s33[q] - nt(w32[q], w32[q]) for q in n]
    x21 = [-nn(x22[q], nn(w21[q], x11[q])) for q in n]
    x33 = inverse_factors(s33)
    for q in n:
        x31 = -nn(x33[q], nn(w31[q], x11[q]) + nn(w32[q], x21[q]))
        x32 = -nn(x33[q], nn(w32[q], x22[q]))
        stores[q][0:B, :] = jnp.concatenate([x11[q], zero, zero], axis=1)
        stores[q][B : 2 * B, :] = jnp.concatenate([x21[q], x22[q], zero], axis=1)
        stores[q][2 * B :, :] = jnp.concatenate([x31, x32, x33[q]], axis=1)


def block(ref, i, j):
    return ref[B * i : B * i + B, B * j : B * j + B]


def diagonal(row):
    r, c = iota2((B, B))
    return jnp.where(r == c, jnp.broadcast_to(row, (B, B)), 0.0)


def lower_of(tri, i, j):
    if i > j:
        return block(tri, i, j)
    r, c = iota2((B, B))
    t = block(tri, i, i)
    return jnp.where(r >= c, t, t.T)


def upper_of(tri, diag, i, j):
    if i > j:
        return block(tri, j, i).T
    r, c = iota2((B, B))
    t = jnp.where(r < c, block(tri, i, i), 0.0)
    return t + t.T + diagonal(diag[:, B * i : B * i + B])


def reduce_arc(x, left_cross, right_cross, rhs, left, right, left_rhs, right_rhs, tri_out, cross_out, vec_out):
    n = x.shape[0]
    nb = n // B
    va = nt(left_cross, x)
    ub = nn(x, right_cross)
    u = nt(rhs, x)
    r, c = iota2((B, B))
    cut = lambda m, i: m[B * i : B * i + B, :]
    col = lambda m, i: m[:, B * i : B * i + B]
    diags = []
    for i in range(nb):
        for j in range(i):
            tri_out[B * i : B * i + B, B * j : B * j + B] = left(i, j) - nt(cut(va, i), cut(va, j))
        ll = left(i, i) - nt(cut(va, i), cut(va, i))
        rr = right(i, i) - tn(col(ub, i), col(ub, i))
        tri_out[B * i : B * i + B, B * i : B * i + B] = jnp.where(r >= c, ll, rr)
        diags.append(jnp.sum(jnp.where(r == c, rr, 0.0), axis=0, keepdims=True))
        for j in range(i + 1, nb):
            tri_out[B * i : B * i + B, B * j : B * j + B] = right(i, j) - tn(col(ub, i), col(ub, j))
    cross_out[...] = -nn(va, ub)
    new_l = left_rhs - nt(u, va)[0:1]
    new_r = right_rhs - nn(u, ub)[0:1]
    pad = jnp.zeros((5, n), f32)
    vec_out[...] = jnp.concatenate([new_l, new_r, jnp.concatenate(diags, axis=1), pad], axis=0)
    return va, ub, u


def gram_kernel(first_ref, second_ref, resid_ref, out_ref):
    links = first_ref.shape[0]
    size = first_ref.shape[2]
    dot = lambda a, b: jnp.dot(a, b, preferred_element_type=f32)
    r, c = iota2((size, size))
    diag = [None] * (links + 1)
    grad = [None] * (links + 1)
    plus = lambda x, y: y if x is None else x + y
    resid = resid_ref[...].astype(f32)
    for i in range(links):
        a = first_ref[i]
        b = second_ref[i]
        at = a.T
        bt = b.T
        e = jnp.broadcast_to(resid[i : i + 1, :], (8, resid.shape[1])).astype(jnp.bfloat16)
        paa = dot(at, a)
        pab = dot(at, b)
        ga = dot(e, a)[0:1]
        diag[i] = plus(diag[i], paa)
        diag[i + 1] = dot(bt, b) - pab - dot(bt, a) + paa
        grad[i] = plus(grad[i], ga)
        grad[i + 1] = dot(e, b)[0:1] - ga
        out_ref[(3 + i) * size : (4 + i) * size, :] = pab - paa
    out_ref[0:size, :] = jnp.where(r >= c, diag[1], diag[3])
    out_ref[2 * size : 3 * size, :] = diag[2]
    d3 = jnp.sum(jnp.where(r == c, diag[3], 0.0), axis=0, keepdims=True)
    out_ref[size : 2 * size, :] = jnp.where(r >= c, diag[0], diag[4])
    d4 = jnp.sum(jnp.where(r == c, diag[4], 0.0), axis=0, keepdims=True)
    rows = [-g for g in grad] + [d3, d4, jnp.zeros((1, size), f32)]
    out_ref[7 * size : 7 * size + 8, :] = jnp.concatenate(rows, axis=0)


def segment_kernel(sums, damp_inner, damp_sep, tri_out, cross_out, vec_out, x_out, va_out, ub_out, u_out, tri_s, cross_s, vec_s):
    size = tri_out.shape[0]
    part = lambda k: sums.at[k * size : (k + 1) * size, :]
    inner, ends, mid = part(0), part(1), part(2)
    cross = [part(3 + k) for k in range(4)]
    row = lambda k: sums[7 * size + k : 7 * size + k + 1, :]
    damp = lambda k, i: diagonal(damp_inner[k : k + 1, B * i : B * i + B])

    def first(i, j):
        s = lower_of(inner, i, j)
        return s + damp(0, i) if i == j else s

    def third(i, j):
        s = upper_of(inner, row(5), i, j)
        return s + damp(2, i) if i == j else s

    factor([first, third], [x_out.at[0], x_out.at[1]])
    zero = jnp.zeros((B, B), f32)
    wide = lambda v: jnp.broadcast_to(v, (8, size))
    none = lambda i, j: zero
    zrow = jnp.zeros((1, size), f32)

    def end(i, j):
        if i < j:
            return block(ends, i, j)
        t = upper_of(ends, row(6), i, i)
        return t + diagonal(damp_sep[:, B * i : B * i + B])

    out = reduce_arc(x_out[0], cross[0][...], cross[1][...], wide(row(1)), lambda i, j: lower_of(ends, i, j), none,
                     row(0), zrow, tri_s.at[0], cross_s.at[0], vec_s.at[0])
    va_out[0], ub_out[0], u_out[0] = out
    out = reduce_arc(x_out[1], cross[2][...], cross[3][...], wide(row(3)), lambda i, j: block(mid, i, j), end,
                     zrow, row(4), tri_s.at[1], cross_s.at[1], vec_s.at[1])
    va_out[1], ub_out[1], u_out[1] = out

    def second(i, j):
        s = upper_of(tri_s.at[0], vec_s[0][2:3], i, j) + lower_of(tri_s.at[1], i, j)
        return s + damp(1, i) if i == j else s

    factor([second], [x_out.at[2]])
    rhs = wide(row(2) + vec_s[0][1:2] + vec_s[1][0:1])
    out = reduce_arc(x_out[2], cross_s[0], cross_s[1], rhs, lambda i, j: lower_of(tri_s.at[0], i, j),
                     lambda i, j: upper_of(tri_s.at[1], vec_s[1][2:3], i, j) if i == j else block(tri_s.at[1], i, j),
                     vec_s[0][0:1], vec_s[1][1:2], tri_out, cross_out, vec_out)
    va_out[2], ub_out[2], u_out[2] = out


def merge_kernel(tri_a, cross_a, vec_a, tri_b, cross_b, vec_b, tri_out, cross_out, vec_out, x):
    size = tri_out.shape[0]

    def shared(i, j):
        return upper_of(tri_a, vec_a[2:3], i, j) + lower_of(tri_b, i, j)

    factor([shared], [x])
    rhs = jnp.broadcast_to(vec_a[1:2] + vec_b[0:1], (8, size))
    reduce_arc(x[...], cross_a[...], cross_b[...], rhs, lambda i, j: lower_of(tri_a, i, j),
               lambda i, j: upper_of(tri_b, vec_b[2:3], i, j) if i == j else block(tri_b, i, j),
               vec_a[0:1], vec_b[1:2], tri_out, cross_out, vec_out)


def closure_kernel(tri, cross, vec, top, x):
    size = tri.shape[0]

    def whole(i, j):
        return (lower_of(tri, i, j) + upper_of(tri, vec[2:3], i, j)) + (block(cross, i, j) + block(cross, j, i).T)

    factor([whole], [x])
    rhs = jnp.broadcast_to(vec[0:1] + vec[1:2], (8, size))
    top[...] = nn(nt(rhs, x[...]), x[...])


def interior_kernel(left, right, x, va, ub, u, out):
    def middle(q, l, r):
        return nn(u[q] - nn(l, va[q]) - nt(r, ub[q]), x[q])

    second = middle(2, left[...], right[...])
    first = middle(0, left[...], second)
    third = middle(1, second, right[...])
    out[...] = jnp.concatenate([first[0:1], second[0:1], third[0:1], jnp.zeros((5, first.shape[1]), f32)], axis=0)


def call(kernel, outs, args, name, scratch=()):
    return pl.pallas_call(
        kernel, out_shape=[jax.ShapeDtypeStruct(s, f32) for s in outs], in_specs=[VMEM] * len(args),
        out_specs=[VMEM] * len(outs), scratch_shapes=[pltpu.VMEM(s, f32) for s in scratch],
        compiler_params=PARAMS, name=name)(*args)


def shift(arrays, by):
    count = lax.axis_size("seg")
    return [lax.ppermute(a, "seg", [(i, (i + by) % count) for i in range(count)]) for a in arrays]


def shards(jac_first, jac_second, residual, damp_inner, damp_sep):
    size = jac_first.shape[-1]
    square, rows = (size, size), (8, size)
    arc_shapes = [square, square, rows]
    (part,) = call(gram_kernel, [(7 * size + 8, size)], (jac_first[0], jac_second[0], residual[0]), "gram")
    sums = lax.psum(part, "band")
    *arc, x, va, ub, u = call(
        segment_kernel, arc_shapes + [(3, *square)] * 3 + [(3, *rows)], (sums, damp_inner[0], damp_sep), "segment",
        [(2, *square), (2, *square), (2, *rows)])
    levels = lax.axis_size("seg").bit_length() - 1
    for level in range(levels):
        other = shift(arc, 1 << level)
        arc = call(merge_kernel, arc_shapes, (*other, *arc), "merge", [square])
    (top,) = call(closure_kernel, [rows], arc, "closure", [square])
    (left,) = shift([top], 1)
    (inner,) = call(interior_kernel, [rows], (left, top, x, va, ub, u), "interior")
    return (top[0:1], inner[None, 0:3])


def solution(mesh):
    return jax.shard_map(
        shards,
        mesh=mesh,
        in_specs=(
            P("seg", None, "band", None),
            P("seg", None, "band", None),
            P("seg", None, "band"),
            P("seg", None, None),
            P("seg", None),
        ),
        out_specs=(P("seg", None), P("seg", None, None)),
        check_vma=False,
    )
```

```python
import functools
import jax
import jax.numpy as jnp
from jax import lax
from jax.experimental import pallas as pl
from jax.experimental.pallas import tpu as pltpu
from jax.sharding import PartitionSpec as P

HIGH = lax.Precision.HIGHEST
B = 128
GROUP = 8
f32 = jnp.float32
VMEM = pl.BlockSpec(memory_space=pltpu.VMEM)
PARAMS = pltpu.CompilerParams(vmem_limit_bytes=48 << 20)


def dg(a, b, ca, cb):
    return lax.dot_general(a, b, (((ca,), (cb,)), ((), ())), precision=HIGH, preferred_element_type=f32)


def nn(a, b):
    return dg(a, b, 1, 0)


def nt(a, b):
    return dg(a, b, 1, 1)


def tn(a, b):
    return dg(a, b, 0, 0)


def iota2(shape):
    return lax.broadcasted_iota(jnp.int32, shape, 0), lax.broadcasted_iota(jnp.int32, shape, 1)


def eliminate_panel(m, k, sub, lane):
    wide = lambda x: jnp.broadcast_to(x, (8, B))
    cols = [wide(m[:, k + j : k + j + 1]) for j in range(8)]
    g = {}
    for j in range(8):
        for i in range(j, 8):
            g[i, j] = g[j, i] = wide(cols[j][i : i + 1, :])
    start = jnp.where((lane >= k) & (lane < k + 8), jnp.where(lane == sub + k, 1.0, 0.0), m)
    r = [wide(start[j : j + 1, :]) for j in range(8)]
    inv = [None] * 8
    pivot_row = [None] * 8
    for j in range(8):
        inv[j] = 1.0 / g[j, j]
        pivot_row[j] = r[j]
        f = {i: g[i, j] * inv[j] for i in range(8) if i != j}
        for i in range(j + 1, 8):
            for h in range(j + 1, i + 1):
                g[i, h] = g[h, i] = g[i, h] - f[i] * g[j, h]
        for i in range(j):
            for h in range(j + 1, 8):
                g[i, h] = g[i, h] - f[i] * g[j, h]
        for i in f:
            r[i] = r[i] - f[i] * r[j]
    y = [r[j] * inv[j] for j in range(8)]
    out = pivot_row[0] * lax.rsqrt(g[0, 0])
    for j in range(1, 8):
        out = jnp.where(sub == j, pivot_row[j] * lax.rsqrt(g[j, j]), out)
    return y, out


def subtract_panel(m, k, y, lane):
    c = [jnp.broadcast_to(m[:, k + j : k + j + 1], (8, B)) for j in range(8)]
    even = c[0] * y[0]
    odd = c[1] * y[1]
    for j in range(2, 8, 2):
        even = even + c[j] * y[j]
        odd = odd + c[j + 1] * y[j + 1]
    return jnp.where((lane >= k) & (lane < k + 8), 0.0, m) - (even + odd)


def inverse_factor(mat):
    sub, lane = iota2((8, B))
    panels = B // 8

    def group(step, m):
        m = list(m)
        for a in range(GROUP):
            k = 8 * a
            y, out = eliminate_panel(m[a], k, sub, lane)
            for i in range(a + 1, panels):
                fresh = subtract_panel(m[i], k, y, lane)
                m[i] = fresh if i < GROUP else jnp.where(i < panels - GROUP * step, fresh, m[i])
            m[a] = jnp.where((lane < k + 8) | (lane >= B - 8 * GROUP * step), out, 0.0)
        m = [pltpu.roll(x, B - 8 * GROUP, 1) for x in m]
        return tuple(m[GROUP:] + m[:GROUP])

    m = tuple(mat[8 * i : 8 * i + 8, :] for i in range(panels))
    return jnp.concatenate(lax.fori_loop(0, panels // GROUP, group, m), axis=0)


def inverse_factors(mats):
    if len(mats) == 1:
        return [inverse_factor(mats[0])]
    sub, lane = iota2((8, B))
    half = B // 2
    wide_lane = lax.broadcasted_iota(jnp.int32, (half, B), 1)

    def eliminate(mats, first):
        mats = [[m[8 * i : 8 * i + 8, :] for i in range(half // 8)] for m in mats]
        for a in range(half // 8):
            k = first + 8 * a
            done = [eliminate_panel(m[a], k, sub, lane) for m in mats]
            for m, (y, out) in zip(mats, done):
                for i in range(a + 1, half // 8):
                    m[i] = subtract_panel(m[i], k, y, lane)
                m[a] = jnp.where((lane < k + 8) | (lane >= first + half), out, 0.0)
        return [jnp.concatenate(m, axis=0) for m in mats]

    tops = eliminate([m[:half] for m in mats], 0)
    rest = [jnp.where(wide_lane < half, 0.0, m[half:]) - tn(t[:, half:], t) for m, t in zip(mats, tops)]
    bottoms = eliminate(rest, half)
    return [jnp.concatenate([jnp.where(wide_lane < half, t, 0.0), b], axis=0) for t, b in zip(tops, bottoms)]


def factor(blocks, stores):
    n = range(len(blocks))
    zero = jnp.zeros((B, B), f32)
    x11 = inverse_factors([blocks[q](0, 0) for q in n])
    w21 = [nt(blocks[q](1, 0), x11[q]) for q in n]
    w31 = [nt(blocks[q](2, 0), x11[q]) for q in n]
    s22 = [blocks[q](1, 1) - nt(w21[q], w21[q]) for q in n]
    s32 = [blocks[q](2, 1) - nt(w31[q], w21[q]) for q in n]
    s33 = [blocks[q](2, 2) - nt(w31[q], w31[q]) for q in n]
    x22 = inverse_factors(s22)
    w32 = [nt(s32[q], x22[q]) for q in n]
    s33 = [s33[q] - nt(w32[q], w32[q]) for q in n]
    x21 = [-nn(x22[q], nn(w21[q], x11[q])) for q in n]
    x33 = inverse_factors(s33)
    for q in n:
        x31 = -nn(x33[q], nn(w31[q], x11[q]) + nn(w32[q], x21[q]))
        x32 = -nn(x33[q], nn(w32[q], x22[q]))
        stores[q][0:B, :] = jnp.concatenate([x11[q], zero, zero], axis=1)
        stores[q][B : 2 * B, :] = jnp.concatenate([x21[q], x22[q], zero], axis=1)
        stores[q][2 * B :, :] = jnp.concatenate([x31, x32, x33[q]], axis=1)


def block(ref, i, j):
    return ref[B * i : B * i + B, B * j : B * j + B]


def diagonal(row):
    r, c = iota2((B, B))
    return jnp.where(r == c, jnp.broadcast_to(row, (B, B)), 0.0)


def lower_of(tri, i, j):
    if i > j:
        return block(tri, i, j)
    r, c = iota2((B, B))
    t = block(tri, i, i)
    return jnp.where(r >= c, t, t.T)


def upper_of(tri, diag, i, j):
    if i > j:
        return block(tri, j, i).T
    r, c = iota2((B, B))
    t = jnp.where(r < c, block(tri, i, i), 0.0)
    return t + t.T + diagonal(diag[:, B * i : B * i + B])


def reduce_arc(x, left_cross, right_cross, rhs, left, right, left_rhs, right_rhs, tri_out, cross_out, vec_out):
    n = x.shape[0]
    nb = n // B
    hi = lambda i: B * (i + 1)
    va = jnp.concatenate([nt(left_cross[:, : hi(i)], x[B * i : hi(i), : hi(i)]) for i in range(nb)], axis=1)
    ub = jnp.concatenate([nn(x[B * i : hi(i), : hi(i)], right_cross[: hi(i)]) for i in range(nb)], axis=0)
    u = nt(rhs, x)
    r, c = iota2((B, B))
    ll = nt(va, va)
    rr = tn(ub, ub)
    cut = lambda m, i, j: m[B * i : B * i + B, B * j : B * j + B]
    diags = []
    for i in range(nb):
        for j in range(i):
            tri_out[B * i : B * i + B, B * j : B * j + B] = left(i, j) - cut(ll, i, j)
        li = left(i, i) - cut(ll, i, i)
        ri = right(i, i) - cut(rr, i, i)
        tri_out[B * i : B * i + B, B * i : B * i + B] = jnp.where(r >= c, li, ri)
        diags.append(jnp.sum(jnp.where(r == c, ri, 0.0), axis=0, keepdims=True))
        for j in range(i + 1, nb):
            tri_out[B * i : B * i + B, B * j : B * j + B] = right(i, j) - cut(rr, i, j)
    cross_out[...] = -nn(va, ub)
    new_l = left_rhs - nt(u, va)[0:1]
    new_r = right_rhs - nn(u, ub)[0:1]
    pad = jnp.zeros((5, n), f32)
    vec_out[...] = jnp.concatenate([new_l, new_r, jnp.concatenate(diags, axis=1), pad], axis=0)
    return va, ub, u


def gram_kernel(first_ref, second_ref, resid_ref, out_ref):
    links = first_ref.shape[0]
    size = first_ref.shape[2]
    dot = lambda a, b: jnp.dot(a, b, preferred_element_type=f32)
    r, c = iota2((size, size))
    diag = [None] * (links + 1)
    grad = [None] * (links + 1)
    plus = lambda x, y: y if x is None else x + y
    resid = resid_ref[...].astype(f32)
    for i in range(links):
        a = first_ref[i]
        b = second_ref[i]
        at = a.T
        bt = b.T
        e = jnp.broadcast_to(resid[i : i + 1, :], (8, resid.shape[1])).astype(jnp.bfloat16)
        paa = dot(at, a)
        pab = dot(at, b)
        ga = dot(e, a)[0:1]
        diag[i] = plus(diag[i], paa)
        diag[i + 1] = dot(bt, b) - pab - dot(bt, a) + paa
        grad[i] = plus(grad[i], ga)
        grad[i + 1] = dot(e, b)[0:1] - ga
        out_ref[(3 + i) * size : (4 + i) * size, :] = pab - paa
    out_ref[0:size, :] = jnp.where(r >= c, diag[1], diag[3])
    out_ref[2 * size : 3 * size, :] = diag[2]
    d3 = jnp.sum(jnp.where(r == c, diag[3], 0.0), axis=0, keepdims=True)
    out_ref[size : 2 * size, :] = jnp.where(r >= c, diag[0], diag[4])
    d4 = jnp.sum(jnp.where(r == c, diag[4], 0.0), axis=0, keepdims=True)
    rows = [-g for g in grad] + [d3, d4, jnp.zeros((1, size), f32)]
    out_ref[7 * size : 7 * size + 8, :] = jnp.concatenate(rows, axis=0)


def views(arc):
    n = arc.shape[-1]
    return arc.at[0:n, :], arc.at[n : 2 * n, :], arc.at[2 * n : 2 * n + 8, :]


def join_arcs(a, b, damp, x, out):
    tri_a, cross_a, vec_a = views(a)
    tri_b, cross_b, vec_b = views(b)

    def shared(i, j):
        s = upper_of(tri_a, vec_a[2:3], i, j) + lower_of(tri_b, i, j)
        return s if damp is None or i != j else s + diagonal(damp[:, B * i : B * i + B])

    factor([shared], [x])
    rhs = jnp.broadcast_to(vec_a[1:2] + vec_b[0:1], (8, a.shape[-1]))
    return reduce_arc(x[...], cross_a[...], cross_b[...], rhs, lambda i, j: lower_of(tri_a, i, j),
                      lambda i, j: upper_of(tri_b, vec_b[2:3], i, j) if i == j else block(tri_b, i, j),
                      vec_a[0:1], vec_b[1:2], *views(out))


def segment_kernel(sums, damp_inner, damp_sep, arc_out, x_out, va_out, ub_out, u_out, arcs):
    size = arc_out.shape[-1]
    part = lambda k: sums.at[k * size : (k + 1) * size, :]
    inner, ends, mid = part(0), part(1), part(2)
    cross = [part(3 + k) for k in range(4)]
    row = lambda k: sums[7 * size + k : 7 * size + k + 1, :]
    damp = lambda k, i: diagonal(damp_inner[k : k + 1, B * i : B * i + B])

    def first(i, j):
        s = lower_of(inner, i, j)
        return s + damp(0, i) if i == j else s

    def third(i, j):
        s = upper_of(inner, row(5), i, j)
        return s + damp(2, i) if i == j else s

    factor([first, third], [x_out.at[0], x_out.at[1]])
    zero = jnp.zeros((B, B), f32)
    wide = lambda v: jnp.broadcast_to(v, (8, size))
    none = lambda i, j: zero
    zrow = jnp.zeros((1, size), f32)

    def end(i, j):
        if i < j:
            return block(ends, i, j)
        t = upper_of(ends, row(6), i, i)
        return t + diagonal(damp_sep[:, B * i : B * i + B])

    out = reduce_arc(x_out[0], cross[0][...], cross[1][...], wide(row(1)), lambda i, j: lower_of(ends, i, j), none,
                     row(0), zrow, *views(arcs.at[0]))
    va_out[0], ub_out[0], u_out[0] = out
    out = reduce_arc(x_out[1], cross[2][...], cross[3][...], wide(row(3)), lambda i, j: block(mid, i, j), end,
                     zrow, row(4), *views(arcs.at[1]))
    va_out[1], ub_out[1], u_out[1] = out
    arcs[1, 2 * size : 2 * size + 1] = arcs[1, 2 * size : 2 * size + 1] + row(2)
    out = join_arcs(arcs.at[0], arcs.at[1], damp_inner[1:2], x_out.at[2], arc_out)
    va_out[2], ub_out[2], u_out[2] = out


def merge_kernel(place, own, *refs):
    *got, out, half_out, x_out, va_out, ub_out, u_out, arcs = refs
    size = own.shape[-1]
    half = size // 2
    core, side = place[0], place[1]
    arcs[side] = own[...]
    if len(got) == 1:
        arcs[1 - side] = got[0][...]
    else:
        near = pl.multiple_of(core * half, 8)
        far = pl.multiple_of((1 - core) * half, 8)
        for at, piece in ((near, got[0]), (far, got[1])):
            arcs[1 - side, pl.ds(at, half), :] = piece[0:half]
            arcs[1 - side, pl.ds(size + at, half), :] = piece[half:size]
        arcs[1 - side, 2 * size :, :] = got[0][size:]
    va_out[...], ub_out[...], u_out[...] = join_arcs(arcs.at[0], arcs.at[1], None, x_out, out)
    mine = pl.multiple_of(core * half, 8)
    half_out[0:half] = out[pl.ds(mine, half), :]
    half_out[half:size] = out[pl.ds(size + mine, half), :]
    half_out[size:] = out[2 * size :]


def solve_kernel(sides, arc, *refs):
    *saved, x_in, va_in, ub_in, u_in, sep_out, inner_out, x = refs
    size = arc.shape[-1]
    tri, cross, vec = views(arc)

    def whole(i, j):
        return (lower_of(tri, i, j) + upper_of(tri, vec[2:3], i, j)) + (block(cross, i, j) + block(cross, j, i).T)

    factor([whole], [x])
    top = nn(nt(jnp.broadcast_to(vec[0:1] + vec[1:2], (8, size)), x[...]), x[...])

    def middle(x, va, ub, u, l, r):
        return nn(u - nn(l, va) - nt(r, ub), x)

    left = right = top
    for level in reversed(range(len(saved) // 4)):
        sx, sva, sub_, su = saved[4 * level : 4 * level + 4]
        mid = middle(sx[...], sva[...], sub_[...], su[...], left, right)
        on_right = sides[level] == 1
        left, right = jnp.where(on_right, mid, left), jnp.where(on_right, right, mid)
    sep_out[...] = right
    inner = lambda q, l, r: middle(x_in[q], va_in[q], ub_in[q], u_in[q], l, r)
    second = inner(2, left, right)
    first = inner(0, left, second)
    third = inner(1, second, right)
    inner_out[...] = jnp.concatenate([first[0:1], second[0:1], third[0:1], jnp.zeros((5, size), f32)], axis=0)


def call(kernel, outs, args, name, scratch=(), scalars=0):
    smem = pl.BlockSpec(memory_space=pltpu.SMEM)
    return pl.pallas_call(
        kernel, out_shape=[jax.ShapeDtypeStruct(s, f32) for s in outs],
        in_specs=[smem] * scalars + [VMEM] * (len(args) - scalars), out_specs=[VMEM] * len(outs),
        scratch_shapes=[pltpu.VMEM(s, f32) for s in scratch], compiler_params=PARAMS, name=name)(*args)


def swap(array, partner):
    count = lax.axis_size("seg")
    return lax.ppermute(array, "seg", [(i, partner(i)) for i in range(count)])


def partner_of(level):
    if level == 0:
        return lambda i: i ^ 1
    if level % 2 == 1:
        return lambda i: i ^ (1 << level)
    return lambda i: i ^ (3 << (level - 1))


def shards(jac_first, jac_second, residual, damp_inner, damp_sep):
    size = jac_first.shape[-1]
    square, rows, whole = (size, size), (8, size), (2 * size + 8, size)
    (part,) = call(gram_kernel, [(7 * size + 8, size)], (jac_first[0], jac_second[0], residual[0]), "gram")
    sums = lax.psum(part, "band")
    arc, *factors = call(
        segment_kernel, [whole] + [(3, *square)] * 3 + [(3, *rows)], (sums, damp_inner[0], damp_sep), "segment",
        [(2, *whole)])
    levels = lax.axis_size("seg").bit_length() - 1
    me = lax.axis_index("seg")
    sides = [(me >> level) & 1 for level in range(levels)]
    saved = []
    for level in range(levels):
        if level == 0:
            got = [swap(arc, partner_of(0))]
        else:
            near = swap(half, partner_of(level))
            got = [near, swap(near, partner_of(0))]
        place = jnp.stack([sides[0], sides[level]]).astype(jnp.int32)
        arc, half, *factor = call(
            merge_kernel, [whole, (size + 8, size)] + [square] * 3 + [rows], (place, arc, *got), "merge", [(2, *whole)], 1)
        saved += factor
    sep, inner = call(
        solve_kernel, [rows, rows], (jnp.stack(sides).astype(jnp.int32), arc, *saved, *factors), "solve", [square], 1)
    return (sep[0:1], inner[None, 0:3])


def solution(mesh):
    return jax.shard_map(
        shards,
        mesh=mesh,
        in_specs=(
            P("seg", None, "band", None),
            P("seg", None, "band", None),
            P("seg", None, "band"),
            P("seg", None, None),
            P("seg", None),
        ),
        out_specs=(P("seg", None), P("seg", None, None)),
        check_vma=False,
    )
```

```python
import functools
import jax
import jax.numpy as jnp
from jax import lax
from jax.experimental import pallas as pl
from jax.experimental.pallas import tpu as pltpu
from jax.sharding import PartitionSpec as P

HIGH = lax.Precision.HIGHEST
B = 128
GROUP = 8
f32 = jnp.float32
VMEM = pl.BlockSpec(memory_space=pltpu.VMEM)
PARAMS = pltpu.CompilerParams(vmem_limit_bytes=48 << 20)


def dg(a, b, ca, cb):
    return lax.dot_general(a, b, (((ca,), (cb,)), ((), ())), precision=HIGH, preferred_element_type=f32)


def nn(a, b):
    return dg(a, b, 1, 0)


def nt(a, b):
    return dg(a, b, 1, 1)


def tn(a, b):
    return dg(a, b, 0, 0)


def iota2(shape):
    return lax.broadcasted_iota(jnp.int32, shape, 0), lax.broadcasted_iota(jnp.int32, shape, 1)


def eliminate_panel(m, k, sub, lane):
    wide = lambda x: jnp.broadcast_to(x, (8, B))
    cols = [wide(m[:, k + j : k + j + 1]) for j in range(8)]
    g = {}
    for j in range(8):
        for i in range(j, 8):
            g[i, j] = g[j, i] = wide(cols[j][i : i + 1, :])
    start = jnp.where((lane >= k) & (lane < k + 8), jnp.where(lane == sub + k, 1.0, 0.0), m)
    r = [wide(start[j : j + 1, :]) for j in range(8)]
    inv = [None] * 8
    pivot_row = [None] * 8
    for j in range(8):
        inv[j] = 1.0 / g[j, j]
        pivot_row[j] = r[j]
        f = {i: g[i, j] * inv[j] for i in range(8) if i != j}
        for i in range(j + 1, 8):
            for h in range(j + 1, i + 1):
                g[i, h] = g[h, i] = g[i, h] - f[i] * g[j, h]
        for i in range(j):
            for h in range(j + 1, 8):
                g[i, h] = g[i, h] - f[i] * g[j, h]
        for i in f:
            r[i] = r[i] - f[i] * r[j]
    y = [r[j] * inv[j] for j in range(8)]
    out = pivot_row[0] * lax.rsqrt(g[0, 0])
    for j in range(1, 8):
        out = jnp.where(sub == j, pivot_row[j] * lax.rsqrt(g[j, j]), out)
    return y, out


def subtract_panel(m, k, y, lane):
    c = [jnp.broadcast_to(m[:, k + j : k + j + 1], (8, B)) for j in range(8)]
    even = c[0] * y[0]
    odd = c[1] * y[1]
    for j in range(2, 8, 2):
        even = even + c[j] * y[j]
        odd = odd + c[j + 1] * y[j + 1]
    return jnp.where((lane >= k) & (lane < k + 8), 0.0, m) - (even + odd)


def inverse_factor(mat):
    sub, lane = iota2((8, B))
    panels = B // 8

    def group(step, m):
        m = list(m)
        for a in range(GROUP):
            k = 8 * a
            y, out = eliminate_panel(m[a], k, sub, lane)
            for i in range(a + 1, panels):
                fresh = subtract_panel(m[i], k, y, lane)
                m[i] = fresh if i < GROUP else jnp.where(i < panels - GROUP * step, fresh, m[i])
            m[a] = jnp.where((lane < k + 8) | (lane >= B - 8 * GROUP * step), out, 0.0)
        m = [pltpu.roll(x, B - 8 * GROUP, 1) for x in m]
        return tuple(m[GROUP:] + m[:GROUP])

    m = tuple(mat[8 * i : 8 * i + 8, :] for i in range(panels))
    return jnp.concatenate(lax.fori_loop(0, panels // GROUP, group, m), axis=0)


def inverse_factors(mats):
    if len(mats) == 1:
        return [inverse_factor(mats[0])]
    sub, lane = iota2((8, B))
    half = B // 2
    wide_lane = lax.broadcasted_iota(jnp.int32, (half, B), 1)

    def eliminate(mats, first):
        mats = [[m[8 * i : 8 * i + 8, :] for i in range(half // 8)] for m in mats]
        for a in range(half // 8):
            k = first + 8 * a
            done = [eliminate_panel(m[a], k, sub, lane) for m in mats]
            for m, (y, out) in zip(mats, done):
                for i in range(a + 1, half // 8):
                    m[i] = subtract_panel(m[i], k, y, lane)
                m[a] = jnp.where((lane < k + 8) | (lane >= first + half), out, 0.0)
        return [jnp.concatenate(m, axis=0) for m in mats]

    tops = eliminate([m[:half] for m in mats], 0)
    rest = [jnp.where(wide_lane < half, 0.0, m[half:]) - tn(t[:, half:], t) for m, t in zip(mats, tops)]
    bottoms = eliminate(rest, half)
    return [jnp.concatenate([jnp.where(wide_lane < half, t, 0.0), b], axis=0) for t, b in zip(tops, bottoms)]


def factor(blocks, stores):
    n = range(len(blocks))
    zero = jnp.zeros((B, B), f32)
    x11 = inverse_factors([blocks[q](0, 0) for q in n])
    w21 = [nt(blocks[q](1, 0), x11[q]) for q in n]
    w31 = [nt(blocks[q](2, 0), x11[q]) for q in n]
    s22 = [blocks[q](1, 1) - nt(w21[q], w21[q]) for q in n]
    s32 = [blocks[q](2, 1) - nt(w31[q], w21[q]) for q in n]
    s33 = [blocks[q](2, 2) - nt(w31[q], w31[q]) for q in n]
    x22 = inverse_factors(s22)
    w32 = [nt(s32[q], x22[q]) for q in n]
    s33 = [s33[q] - nt(w32[q], w32[q]) for q in n]
    x21 = [-nn(x22[q], nn(w21[q], x11[q])) for q in n]
    x33 = inverse_factors(s33)
    for q in n:
        x31 = -nn(x33[q], nn(w31[q], x11[q]) + nn(w32[q], x21[q]))
        x32 = -nn(x33[q], nn(w32[q], x22[q]))
        stores[q][0:B, :] = jnp.concatenate([x11[q], zero, zero], axis=1)
        stores[q][B : 2 * B, :] = jnp.concatenate([x21[q], x22[q], zero], axis=1)
        stores[q][2 * B :, :] = jnp.concatenate([x31, x32, x33[q]], axis=1)


def block(ref, i, j):
    return ref[B * i : B * i + B, B * j : B * j + B]


def diagonal(row):
    r, c = iota2((B, B))
    return jnp.where(r == c, jnp.broadcast_to(row, (B, B)), 0.0)


def lower_of(tri, i, j):
    if i > j:
        return block(tri, i, j)
    r, c = iota2((B, B))
    t = block(tri, i, i)
    return jnp.where(r >= c, t, t.T)


def upper_of(tri, diag, i, j):
    if i > j:
        return block(tri, j, i).T
    r, c = iota2((B, B))
    t = jnp.where(r < c, block(tri, i, i), 0.0)
    return t + t.T + diagonal(diag[:, B * i : B * i + B])


def reduce_arc(x, left_cross, right_cross, rhs, left, right, left_rhs, right_rhs, tri_out, cross_out, vec_out):
    n = x.shape[0]
    nb = n // B
    hi = lambda i: B * (i + 1)
    va = jnp.concatenate([nt(left_cross[:, : hi(i)], x[B * i : hi(i), : hi(i)]) for i in range(nb)], axis=1)
    ub = jnp.concatenate([nn(x[B * i : hi(i), : hi(i)], right_cross[: hi(i)]) for i in range(nb)], axis=0)
    u = nt(rhs, x)
    r, c = iota2((B, B))
    ll = nt(va, va)
    rr = tn(ub, ub)
    cut = lambda m, i, j: m[B * i : B * i + B, B * j : B * j + B]
    diags = []
    for i in range(nb):
        for j in range(i):
            tri_out[B * i : B * i + B, B * j : B * j + B] = left(i, j) - cut(ll, i, j)
        li = left(i, i) - cut(ll, i, i)
        ri = right(i, i) - cut(rr, i, i)
        tri_out[B * i : B * i + B, B * i : B * i + B] = jnp.where(r >= c, li, ri)
        diags.append(jnp.sum(jnp.where(r == c, ri, 0.0), axis=0, keepdims=True))
        for j in range(i + 1, nb):
            tri_out[B * i : B * i + B, B * j : B * j + B] = right(i, j) - cut(rr, i, j)
    cross_out[...] = -nn(va, ub)
    new_l = left_rhs - nt(u, va)[0:1]
    new_r = right_rhs - nn(u, ub)[0:1]
    pad = jnp.zeros((5, n), f32)
    vec_out[...] = jnp.concatenate([new_l, new_r, jnp.concatenate(diags, axis=1), pad], axis=0)
    return va, ub, u


def gram_kernel(first_ref, second_ref, resid_ref, out_ref):
    links = first_ref.shape[0]
    size = first_ref.shape[2]
    dot = lambda a, b: jnp.dot(a, b, preferred_element_type=f32)
    r, c = iota2((size, size))
    diag = [None] * (links + 1)
    grad = [None] * (links + 1)
    plus = lambda x, y: y if x is None else x + y
    resid = resid_ref[...].astype(f32)
    for i in range(links):
        a = first_ref[i]
        b = second_ref[i]
        at = a.T
        bt = b.T
        e = jnp.broadcast_to(resid[i : i + 1, :], (8, resid.shape[1])).astype(jnp.bfloat16)
        paa = dot(at, a)
        pab = dot(at, b)
        ga = dot(e, a)[0:1]
        diag[i] = plus(diag[i], paa)
        diag[i + 1] = dot(bt, b) - pab - dot(bt, a) + paa
        grad[i] = plus(grad[i], ga)
        grad[i + 1] = dot(e, b)[0:1] - ga
        out_ref[(3 + i) * size : (4 + i) * size, :] = pab - paa
    out_ref[0:size, :] = jnp.where(r >= c, diag[1], diag[3])
    out_ref[2 * size : 3 * size, :] = diag[2]
    d3 = jnp.sum(jnp.where(r == c, diag[3], 0.0), axis=0, keepdims=True)
    out_ref[size : 2 * size, :] = jnp.where(r >= c, diag[0], diag[4])
    d4 = jnp.sum(jnp.where(r == c, diag[4], 0.0), axis=0, keepdims=True)
    rows = [-g for g in grad] + [d3, d4, jnp.zeros((1, size), f32)]
    out_ref[7 * size : 7 * size + 8, :] = jnp.concatenate(rows, axis=0)


def views(arc):
    n = arc.shape[-1]
    return arc.at[0:n, :], arc.at[n : 2 * n, :], arc.at[2 * n : 2 * n + 8, :]


def join_arcs(a, b, damp, x, out):
    tri_a, cross_a, vec_a = views(a)
    tri_b, cross_b, vec_b = views(b)

    def shared(i, j):
        s = upper_of(tri_a, vec_a[2:3], i, j) + lower_of(tri_b, i, j)
        return s if damp is None or i != j else s + diagonal(damp[:, B * i : B * i + B])

    factor([shared], [x])
    rhs = jnp.broadcast_to(vec_a[1:2] + vec_b[0:1], (8, a.shape[-1]))
    return reduce_arc(x[...], cross_a[...], cross_b[...], rhs, lambda i, j: lower_of(tri_a, i, j),
                      lambda i, j: upper_of(tri_b, vec_b[2:3], i, j) if i == j else block(tri_b, i, j),
                      vec_a[0:1], vec_b[1:2], *views(out))


def segment_kernel(sums, damp_inner, damp_sep, arc_out, x_out, va_out, ub_out, u_out, arcs):
    size = arc_out.shape[-1]
    part = lambda k: sums.at[k * size : (k + 1) * size, :]
    inner, ends, mid = part(0), part(1), part(2)
    cross = [part(3 + k) for k in range(4)]
    row = lambda k: sums[7 * size + k : 7 * size + k + 1, :]
    damp = lambda k, i: diagonal(damp_inner[k : k + 1, B * i : B * i + B])

    def first(i, j):
        s = lower_of(inner, i, j)
        return s + damp(0, i) if i == j else s

    def third(i, j):
        s = upper_of(inner, row(5), i, j)
        return s + damp(2, i) if i == j else s

    factor([first, third], [x_out.at[0], x_out.at[1]])
    zero = jnp.zeros((B, B), f32)
    wide = lambda v: jnp.broadcast_to(v, (8, size))
    none = lambda i, j: zero
    zrow = jnp.zeros((1, size), f32)

    def end(i, j):
        if i < j:
            return block(ends, i, j)
        t = upper_of(ends, row(6), i, i)
        return t + diagonal(damp_sep[:, B * i : B * i + B])

    out = reduce_arc(x_out[0], cross[0][...], cross[1][...], wide(row(1)), lambda i, j: lower_of(ends, i, j), none,
                     row(0), zrow, *views(arcs.at[0]))
    va_out[0], ub_out[0], u_out[0] = out
    out = reduce_arc(x_out[1], cross[2][...], cross[3][...], wide(row(3)), lambda i, j: block(mid, i, j), end,
                     zrow, row(4), *views(arcs.at[1]))
    va_out[1], ub_out[1], u_out[1] = out
    arcs[1, 2 * size : 2 * size + 1] = arcs[1, 2 * size : 2 * size + 1] + row(2)
    out = join_arcs(arcs.at[0], arcs.at[1], damp_inner[1:2], x_out.at[2], arc_out)
    va_out[2], ub_out[2], u_out[2] = out


def merge_kernel(place, own, *refs):
    *got, out, half_out, x_out, va_out, ub_out, u_out, arcs = refs
    size = own.shape[-1]
    half = size // 2
    core, side = place[0], place[1]
    arcs[side] = own[...]
    if len(got) == 1:
        arcs[1 - side] = got[0][...]
    else:
        near = pl.multiple_of(core * half, 8)
        far = pl.multiple_of((1 - core) * half, 8)
        for at, piece in ((near, got[0]), (far, got[1])):
            arcs[1 - side, pl.ds(at, half), :] = piece[0:half]
            arcs[1 - side, pl.ds(size + at, half), :] = piece[half:size]
        arcs[1 - side, 2 * size :, :] = got[0][size:]
    va_out[...], ub_out[...], u_out[...] = join_arcs(arcs.at[0], arcs.at[1], None, x_out, out)
    mine = pl.multiple_of(core * half, 8)
    half_out[0:half] = out[pl.ds(mine, half), :]
    half_out[half:size] = out[pl.ds(size + mine, half), :]
    half_out[size:] = out[2 * size :]


def solve_kernel(sides, arc, *refs):
    far, refs = refs[: len(refs) // 2 - 2], refs[len(refs) // 2 - 2 :]
    sep_out, inner_out, x, *near, sems = refs
    size = arc.shape[-1]
    copies = [pltpu.make_async_copy(f, n, sems.at[i]) for i, (f, n) in enumerate(zip(far, near))]
    for copy in copies:
        copy.start()
    *saved, x_in, va_in, ub_in, u_in = near
    tri, cross, vec = views(arc)

    def whole(i, j):
        return (lower_of(tri, i, j) + upper_of(tri, vec[2:3], i, j)) + (block(cross, i, j) + block(cross, j, i).T)

    factor([whole], [x])
    top = nn(nt(jnp.broadcast_to(vec[0:1] + vec[1:2], (8, size)), x[...]), x[...])

    for copy in copies:
        copy.wait()

    def middle(x, va, ub, u, l, r):
        return nn(u - nn(l, va) - nt(r, ub), x)

    left = right = top
    for level in reversed(range(len(saved) // 4)):
        sx, sva, sub_, su = saved[4 * level : 4 * level + 4]
        mid = middle(sx[...], sva[...], sub_[...], su[...], left, right)
        on_right = sides[level] == 1
        left, right = jnp.where(on_right, mid, left), jnp.where(on_right, right, mid)
    sep_out[...] = right
    inner = lambda q, l, r: middle(x_in[q], va_in[q], ub_in[q], u_in[q], l, r)
    second = inner(2, left, right)
    first = inner(0, left, second)
    third = inner(1, second, right)
    inner_out[...] = jnp.concatenate([first[0:1], second[0:1], third[0:1], jnp.zeros((5, size), f32)], axis=0)


def call(kernel, outs, args, name, scratch=(), scalars=0):
    smem = pl.BlockSpec(memory_space=pltpu.SMEM)
    return pl.pallas_call(
        kernel, out_shape=[jax.ShapeDtypeStruct(s, f32) for s in outs],
        in_specs=[smem] * scalars + [VMEM] * (len(args) - scalars), out_specs=[VMEM] * len(outs),
        scratch_shapes=[pltpu.VMEM(s, f32) for s in scratch], compiler_params=PARAMS, name=name)(*args)


def swap(array, partner):
    count = lax.axis_size("seg")
    return lax.ppermute(array, "seg", [(i, partner(i)) for i in range(count)])


def partner_of(level):
    if level == 0:
        return lambda i: i ^ 1
    if level % 2 == 1:
        return lambda i: i ^ (1 << level)
    return lambda i: i ^ (3 << (level - 1))


def shards(jac_first, jac_second, residual, damp_inner, damp_sep):
    size = jac_first.shape[-1]
    square, rows, whole = (size, size), (8, size), (2 * size + 8, size)
    (part,) = call(gram_kernel, [(7 * size + 8, size)], (jac_first[0], jac_second[0], residual[0]), "gram")
    sums = lax.psum(part, "band")
    arc, *factors = call(
        segment_kernel, [whole] + [(3, *square)] * 3 + [(3, *rows)], (sums, damp_inner[0], damp_sep), "segment",
        [(2, *whole)])
    levels = lax.axis_size("seg").bit_length() - 1
    me = lax.axis_index("seg")
    sides = [(me >> level) & 1 for level in range(levels)]
    saved = []
    for level in range(levels):
        if level == 0:
            got = [swap(arc, partner_of(0))]
        else:
            near = swap(half, partner_of(level))
            got = [near, swap(near, partner_of(0))]
        place = jnp.stack([sides[0], sides[level]]).astype(jnp.int32)
        arc, half, *factor = call(
            merge_kernel, [whole, (size + 8, size)] + [square] * 3 + [rows], (place, arc, *got), "merge", [(2, *whole)], 1)
        saved += factor
    kept = [*saved, *factors]
    near = [pltpu.VMEM(k.shape, f32) for k in kept] + [pltpu.SemaphoreType.DMA((len(kept),))]
    sep, inner = pl.pallas_call(
        solve_kernel, out_shape=[jax.ShapeDtypeStruct(rows, f32)] * 2,
        in_specs=[pl.BlockSpec(memory_space=pltpu.SMEM), VMEM] + [pl.BlockSpec(memory_space=pltpu.HBM)] * len(kept),
        out_specs=[VMEM] * 2, scratch_shapes=[pltpu.VMEM(square, f32)] + near,
        compiler_params=pltpu.CompilerParams(vmem_limit_bytes=60 << 20), name="solve",
    )(jnp.stack(sides).astype(jnp.int32), arc, *kept)
    return (sep[0:1], inner[None, 0:3])


def solution(mesh):
    return jax.shard_map(
        shards,
        mesh=mesh,
        in_specs=(
            P("seg", None, "band", None),
            P("seg", None, "band", None),
            P("seg", None, "band"),
            P("seg", None, None),
            P("seg", None),
        ),
        out_specs=(P("seg", None), P("seg", None, None)),
        check_vma=False,
    )
```
